128 devices in a mesh: own: 128 (over z, x, y, core).
Axes of the slice: x: 4, y: 4, z: 4, core: 2. Of those that a mesh axis runs over, the one named last changes fastest.
Arguments:
- sentence_vectors: bfloat16 [65536, 1024], P('own'), may hold values from -12 to 12
- group_assignment: int32 [65536, 1], P('own'), may hold values from 0 to 511; in each aligned block of 512 rows (0 to 511, 512 to 1023, ...) at most 2 rows name the same one
- adjacent_importance: bfloat16 [65536], P('own'), may hold values from 0.099609375 to 10
- group_sharpness: bfloat16 [512], P('own'), may hold values from 8 to 32
Outputs:
- smoothed: bfloat16 [65536, 1024], P('own')
- dup_score: bfloat16 [65536], P('own')
The draws below stay inside these ranges and needn't reach their ends.
Inputs may be any that keep to these rules, and one draw needn't show every extreme that they name: `group_assignment`: of the rows of one device, at most 2 name the same cluster; every cluster is named by some row.
All inputs are finite; a program needn't handle non-finite values.
Results may differ from the reference program's by a relative error of at most 0.0056.
Values may be sent and summed in bfloat16 or wider, within the bound.
No kernel may reach another device: no remote copies, remote signals or barrier semaphores. Data moves between devices by JAX's collectives and lax.ppermute only.
A program may use at most 64 MiB of HBM per device.

```python
import math
import jax
import jax.numpy as jnp
import numpy as np
from jax import lax

D = 1024
ROWS_DEV = 512
GROUP_COUNT = 512
CAP = 2
SLOTS = 256
ROWS = 65536
N_OWN = 128


def level_of(own_key, dims, shards, low, high):
    gain, own = 1.0, jax.random.fold_in(own_key, 6)
    for dim, shards_of in shards:
        steps = jnp.exp(jax.random.uniform(jax.random.fold_in(own, dim), (shards_of,), jnp.float32, low / len(shards), high / len(shards)))
        gain = gain * jnp.repeat(steps, dims[dim] // shards_of).reshape([-1 if axis == dim else 1 for axis in range(len(dims))])
    return gain


def assign_block(own_key, own, number, rows, count, top, limit, skew):
    sequence = jax.random.permutation(own_key, count)
    heavy_load, ordinary = load_shares(count, rows * top, limit, skew, True), load_shares(count, rows * top, limit, skew, False)
    places = jnp.arange(count)

    def named(lengths, turn):
        used = int((lengths > 0).sum())
        fixed = max(1, used // 4)
        passed = fixed + (places - fixed + turn * (used - fixed)) % max(1, count - fixed)
        return jnp.zeros((count,), jnp.int32).at[sequence[jnp.where(places < fixed, places, passed)]].set(jnp.asarray(lengths, jnp.int32))

    lengths = jnp.where(number % 4 == 0, named(heavy_load, number // 4), named(ordinary, number - number // 4 - 1))
    mixed = jax.random.permutation(jax.random.fold_in(own, 3), count)
    giver, taker = mixed[0:count // 2 * 2:2], mixed[1:count // 2 * 2:2]
    room = jnp.minimum(lengths[giver] - 1, limit - lengths[taker]) // 2
    room = jnp.where((giver == sequence[0]) | (taker == sequence[0]) | (lengths[taker] == 0), 0, jnp.maximum(room, 0))
    passed = jax.random.randint(jax.random.fold_in(own, 4), (count // 2,), 0, 1 << 20) % (room + 1)
    lengths = lengths.at[giver].add(-passed).at[taker].add(passed)
    labels = jnp.searchsorted(jnp.cumsum(lengths), jnp.arange(rows * top), side="right").astype(jnp.int32)
    table = labels.reshape(top, rows).T
    table = table[jax.random.permutation(jax.random.fold_in(own, 1), rows)]
    turn = jax.random.randint(jax.random.fold_in(own, 2), (rows, 1), 0, top)
    return jnp.take_along_axis(table, (jnp.arange(top)[None, :] + turn) % top, axis=1)


def load_shares(count, total, bound, skew, full):
    portions = [(1 << 20) // math.isqrt(grade ** skew) + 1 for grade in range(1, count + 1)]
    largest = bound if full else min(bound, max(-(-total // count), total * portions[0] // sum(portions)))
    least = 1 if total - largest >= count - 1 else 0
    counts, surplus = [largest] + [least] * (count - 1), total - largest - least * (count - 1)
    while surplus > 0:
        candidates = [i for i in range(1, count) if counts[i] < largest] or [i for i in range(1, count) if counts[i] < bound]
        mass, budget = sum([portions[i] for i in candidates]), surplus
        for i in candidates:
            more = min(bound - counts[i], max(1, budget * portions[i] // mass), surplus)
            counts[i] = counts[i] + more
            surplus = surplus - more
    return np.array(counts)


def noise(rng, extent, scale, reach, pieces=(), held_as=jnp.bfloat16):
    drawn = jax.random.normal(rng, extent, jnp.float32) * scale
    if len(pieces) > 0:
        drawn = level_of(rng, extent, pieces, -0.22, 0.18) * drawn
    return jnp.clip(drawn, min=-reach, max=reach).astype(held_as)


def setup_inputs(seed: int = 0) -> dict:
    seeds = jax.random.split(jax.random.key(seed), 5)
    sentence_vectors = noise(seeds[0], (ROWS, D), 3.0, 12.0, ((0, 128),))
    group_assignment_keys = jax.random.split(jax.random.fold_in(seeds[1], 1), ROWS // ROWS_DEV)
    group_assignment_turns = jax.random.permutation(jax.random.fold_in(seeds[1], 3), ROWS // ROWS_DEV)
    group_assignment = jax.vmap(lambda own, number: assign_block(jax.random.fold_in(seeds[1], 2), own, number, ROWS_DEV, GROUP_COUNT, 1, CAP, 2))(group_assignment_keys, group_assignment_turns).reshape((ROWS, 1))
    adjacent_importance = jnp.clip(jnp.exp(math.log(10.0) - 4.609084 * jax.random.uniform(seeds[2], (ROWS,), jnp.float32) ** level_of(seeds[2], (ROWS,), ((0, 128),), -0.2, 0.2)), 0.099609375, 10.0).astype(jnp.bfloat16)
    group_sharpness = jnp.clip(jnp.exp(math.log(32.0) - 1.3862944 * jax.random.uniform(seeds[3], (GROUP_COUNT,), jnp.float32) ** level_of(seeds[3], (GROUP_COUNT,), ((0, 128),), -0.2, 0.2)), 8.0, 32.0).astype(jnp.bfloat16)
    return dict(sentence_vectors=sentence_vectors, group_assignment=group_assignment, adjacent_importance=adjacent_importance, group_sharpness=group_sharpness)


def smooth_rows(key_rows, slot_weights, exponent_sharpness, start, count):
    widened = key_rows.astype(jnp.float32)
    square_sum = lax.optimization_barrier(jnp.sum(widened * widened, axis=1))
    unit_rows = (widened * lax.rsqrt(square_sum + 1e-06)[:, None]).astype(jnp.bfloat16)
    queries = lax.dynamic_slice_in_dim(unit_rows, start, count, 0)
    cosine = lax.dot_general(queries, unit_rows, (((1,), (1,)), ((), ())), preferred_element_type=jnp.float32)
    positions = start + jnp.arange(count, dtype=jnp.int32)
    columns = jnp.arange(key_rows.shape[0], dtype=jnp.int32)
    cosine = jnp.where(positions[:, None] == columns[None, :], jnp.float32(0.0), cosine)
    expo = slot_weights.astype(jnp.float32)[None, :] * jnp.exp(exponent_sharpness * (cosine - 1.0))
    totals = lax.optimization_barrier(jnp.sum(expo, axis=1))
    numer = jnp.dot(expo.astype(jnp.bfloat16), key_rows, preferred_element_type=jnp.float32)
    return ((numer / totals[:, None]).astype(jnp.bfloat16), (jnp.log(totals) + exponent_sharpness).astype(jnp.bfloat16))

def block_ranks(ident):
    order = jnp.argsort(ident, stable=True).astype(jnp.int32)
    ordered = ident[order]
    firsts = jnp.searchsorted(ordered, ordered, side='left').astype(jnp.int32)
    ranked = jnp.arange(ident.shape[0], dtype=jnp.int32) - firsts
    return jnp.zeros(ident.shape, jnp.int32).at[order].set(ranked)

def reference(sentence_vectors, group_assignment, adjacent_importance, group_sharpness):
    ident = group_assignment[:, 0].astype(jnp.int32)
    ranks_all = jax.vmap(block_ranks)(ident.reshape(N_OWN, ROWS_DEV)).reshape(-1)
    source = jnp.arange(ROWS, dtype=jnp.int32) // ROWS_DEV
    position = source * CAP + ranks_all
    table = jnp.full((GROUP_COUNT, SLOTS), ROWS, jnp.int32).at[ident, position].set(jnp.arange(ROWS, dtype=jnp.int32))
    padded = jnp.concatenate([sentence_vectors, jnp.zeros((1, D), jnp.bfloat16)], axis=0)
    padded_weight = jnp.concatenate([adjacent_importance, jnp.zeros((1,), jnp.bfloat16)], axis=0)

    def one_cluster(carry, belongs_indicator):
        smooth_all, score_all = carry
        index_row = table[belongs_indicator]
        key_rows = padded[index_row]
        slot_weights = padded_weight[index_row]
        exponent_sharpness = group_sharpness[belongs_indicator].astype(jnp.float32)
        smooth_partial, score_part = smooth_rows(key_rows, slot_weights, exponent_sharpness, 0, SLOTS)
        return ((smooth_all.at[index_row].set(smooth_partial), score_all.at[index_row].set(score_part)), None)
    start_carry = (jnp.zeros((ROWS + 1, D), jnp.bfloat16), jnp.zeros((ROWS + 1,), jnp.bfloat16))
    (smooth_all, score_all), _ = lax.scan(one_cluster, start_carry, jnp.arange(GROUP_COUNT, dtype=jnp.int32))
    return (smooth_all[:ROWS], score_all[:ROWS])
```

```python
import jax
import jax.numpy as jnp
from jax import lax
from jax.experimental import pallas as pl
from jax.experimental.pallas import tpu as pltpu
from jax.sharding import PartitionSpec as P

F32 = jnp.float32
BF16 = jnp.bfloat16
LANES = 128
CAP = 2


def iota(shape, dim):
    return lax.broadcasted_iota(jnp.int32, shape, dim)


def column_of(row):
    count = row.shape[1]
    parts = []
    for start in range(0, count, LANES):
        wide = jnp.broadcast_to(row[:, start : start + LANES], (LANES, LANES))
        parts.append(jnp.transpose(wide))
    return jnp.concatenate(parts, axis=0)


def row_of(column):
    count = column.shape[0]
    parts = []
    for start in range(0, count, LANES):
        parts.append(jnp.transpose(column[start : start + LANES, :])[0:1, :])
    return jnp.concatenate(parts, axis=1)


def dot(a, b, contract=((1,), (0,))):
    return lax.dot_general(a, b, (contract, ((), ())), preferred_element_type=F32)


def pack_kernel(ident_ref, weight_ref, rows_ref, send_ref, slot_ref):
    count = rows_ref.shape[0]
    width = rows_ref.shape[1]
    slots = send_ref.shape[0]
    ident = ident_ref[...]
    ident_col = column_of(ident)
    ranks = []
    for start in range(0, count, LANES):
        here = ident[:, start : start + LANES]
        same = ident_col == here
        earlier = iota((count, LANES), 0) < iota((count, LANES), 1) + start
        ranks.append(jnp.sum((same & earlier).astype(jnp.int32), axis=0, keepdims=True))
    slot = CAP * ident + jnp.concatenate(ranks, axis=1)
    slot_ref[...] = slot
    weight_col = column_of(weight_ref[...].astype(F32)).astype(BF16)
    block = 256

    for index in range(slots // block):
        start = index * block
        hot = (slot == start + iota((block, count), 0)).astype(BF16)
        send_ref[start : start + block, 0:width] = dot(hot, rows_ref[...]).astype(BF16)
        send_ref[start : start + block, width : width + LANES] = dot(hot, weight_col).astype(BF16)


def pack(ident, weight, rows, slots):
    count, width = rows.shape
    vmem = pl.BlockSpec(memory_space=pltpu.VMEM)
    return pl.pallas_call(
        pack_kernel,
        out_shape=(
            jax.ShapeDtypeStruct((slots, width + LANES), BF16),
            jax.ShapeDtypeStruct((1, count), jnp.int32),
        ),
        in_specs=[vmem] * 3,
        out_specs=(vmem, vmem),
        cost_estimate=pl.CostEstimate(
            flops=2 * slots * count * (width + LANES), bytes_accessed=4 << 20, transcendentals=0
        ),
        compiler_params=pltpu.CompilerParams(vmem_limit_bytes=12 << 20),
        name="pack",
    )(ident, weight, rows)


def hot_kernel(slot_ref, hot_ref):
    count, slots = hot_ref.shape
    slot_col = column_of(slot_ref[...])
    for start in range(0, slots, LANES):
        hot_ref[:, start : start + LANES] = (slot_col == start + iota((count, LANES), 1)).astype(BF16)


def hot_rows(slot, slots):
    count = slot.shape[1]
    vmem = pl.BlockSpec(memory_space=pltpu.VMEM)
    return pl.pallas_call(
        hot_kernel,
        out_shape=jax.ShapeDtypeStruct((count, slots), BF16),
        in_specs=[vmem],
        out_specs=vmem,
        cost_estimate=pl.CostEstimate(flops=count * slots, bytes_accessed=1 << 20, transcendentals=0),
        compiler_params=pltpu.CompilerParams(vmem_limit_bytes=8 << 20),
        name="hot_rows",
    )(slot)


def cluster_kernel(sharp_ref, got_ref, back_ref, rows_s, unit_s, weight_s, done_s):
    members = sharp_ref.shape[1]
    slots, wide = got_ref.shape
    width = wide - LANES
    block = 256
    share = members * CAP
    group = block // members
    new, old = iota((block, block), 0), iota((block, block), 1)
    from_old = (new % group) // CAP * share + new // group * CAP + new % CAP
    perm = (from_old == old).astype(BF16)
    from_new = (old % group) // CAP * share + old // group * CAP + old % CAP
    unperm = (from_new == new).astype(BF16)

    for index in range(slots // block):
        taken = got_ref[index * block : (index + 1) * block, :]
        moved = dot(perm, taken[:, 0:width])
        weight = dot(perm, taken[:, width:wide])
        square_sum = jnp.sum(moved * moved, axis=1, keepdims=True)
        unit = (moved * lax.rsqrt(square_sum + 1e-06)).astype(BF16)
        moved = moved.astype(BF16)
        for member in range(members):
            at = member * slots // members + index * group
            of = slice(member * group, (member + 1) * group)
            rows_s[at : at + group, :] = moved[of, :]
            unit_s[at : at + group, :] = unit[of, :]
            weight_s[at : at + group, :] = weight[of, :]

    each = slots // members
    same = iota((each, each), 0) == iota((each, each), 1)
    for member in range(members):
        of = slice(member * each, (member + 1) * each)
        sharp = sharp_ref[0, member]
        unit = unit_s[of, :]
        cosine = jnp.where(same, F32(0.0), dot(unit, unit, ((1,), (1,))))
        expo = row_of(weight_s[of, :]) * jnp.exp(sharp * (cosine - 1.0))
        total = jnp.sum(expo, axis=1, keepdims=True)
        numer = dot(expo.astype(BF16), rows_s[of, :])
        done_s[of, 0:width] = (numer * (1.0 / total)).astype(BF16)
        score = (jnp.log(total) + sharp).astype(BF16)
        done_s[of, width:wide] = jnp.broadcast_to(score, (each, LANES))

    for index in range(slots // block):
        parts = []
        for member in range(members):
            at = member * each + index * group
            parts.append(done_s[at : at + group, :])
        done = jnp.concatenate(parts, axis=0)
        back_ref[index * block : (index + 1) * block, :] = dot(unperm, done).astype(BF16)


def clusters(sharp, got):
    slots, wide = got.shape
    vmem = pl.BlockSpec(memory_space=pltpu.VMEM)
    return pl.pallas_call(
        cluster_kernel,
        out_shape=jax.ShapeDtypeStruct((slots, wide), BF16),
        in_specs=[pl.BlockSpec(memory_space=pltpu.SMEM), vmem],
        out_specs=vmem,
        scratch_shapes=[
            pltpu.VMEM((slots, wide - LANES), BF16),
            pltpu.VMEM((slots, wide - LANES), BF16),
            pltpu.VMEM((slots, LANES), F32),
            pltpu.VMEM((slots, wide), BF16),
        ],
        compiler_params=pltpu.CompilerParams(vmem_limit_bytes=20 << 20),
        name="clusters",
    )(sharp, got)


def home_kernel(hot_ref, home_ref, smooth_ref, score_ref):
    count, width = smooth_ref.shape
    block = 256
    for start in range(0, count, block):
        hot = hot_ref[start : start + block, :]
        smooth_ref[start : start + block, :] = dot(hot, home_ref[:, 0:width]).astype(BF16)
        score = row_of(dot(hot, home_ref[:, width : width + LANES]))
        score_ref[:, start : start + block] = score.astype(BF16)


def bring_home(hot, home):
    count = hot.shape[0]
    width = home.shape[1] - LANES
    vmem = pl.BlockSpec(memory_space=pltpu.VMEM)
    return pl.pallas_call(
        home_kernel,
        out_shape=(
            jax.ShapeDtypeStruct((count, width), BF16),
            jax.ShapeDtypeStruct((1, count), BF16),
        ),
        in_specs=[vmem] * 2,
        out_specs=(vmem, vmem),
        compiler_params=pltpu.CompilerParams(vmem_limit_bytes=12 << 20),
        name="bring_home",
    )(hot, home)


def local(sentence_vectors, group_assignment, adjacent_importance, group_sharpness):
    devices = lax.axis_size("own")
    local_entries = group_sharpness.shape[0]
    row_count = sentence_vectors.shape[0]
    slots = devices * local_entries * CAP
    send, slot = pack(
        group_assignment.reshape(1, row_count),
        adjacent_importance.reshape(1, row_count),
        sentence_vectors,
        slots,
    )
    got = lax.all_to_all(send, "own", split_axis=0, concat_axis=0, tiled=True)
    sharp = group_sharpness.astype(F32).reshape(1, local_entries)
    back = clusters(sharp, got)
    hot = hot_rows(slot, slots)
    home = lax.all_to_all(back, "own", split_axis=0, concat_axis=0, tiled=True)
    smoothed, score = bring_home(hot, home)
    return (smoothed, score.reshape(row_count))


def solution(mesh):
    placed = (P("own", None), P("own", None), P("own"), P("own"))
    return jax.shard_map(
        local, mesh=mesh, in_specs=placed, out_specs=(P("own", None), P("own")), check_vma=False
    )
```

```python
import jax
import jax.numpy as jnp
from jax import lax
from jax.experimental import pallas as pl
from jax.experimental.pallas import tpu as pltpu
from jax.sharding import PartitionSpec as P

F32 = jnp.float32
BF16 = jnp.bfloat16
LANES = 128
CAP = 2
BLOCK = 256
PARTS = 2
LOG2_E = 1.4426950408889634
MIB = 1 << 20
IN_VMEM = pl.BlockSpec(memory_space=pltpu.VMEM)
IN_SMEM = pl.BlockSpec(memory_space=pltpu.SMEM)
IN_HBM = pl.BlockSpec(memory_space=pltpu.HBM)


def iota(shape, dim):
    return lax.broadcasted_iota(jnp.int32, shape, dim)


def dot(a, b, contract=((1,), (0,))):
    return lax.dot_general(a, b, (contract, ((), ())), preferred_element_type=F32)


def column_of(row):
    parts = []
    for start in range(0, row.shape[1], LANES):
        wide = jnp.broadcast_to(row[:, start : start + LANES], (LANES, LANES))
        parts.append(jnp.transpose(wide))
    return jnp.concatenate(parts, axis=0)


def turned(tall):
    parts = []
    for start in range(0, tall.shape[0], LANES):
        parts.append(jnp.transpose(tall[start : start + LANES, :]))
    return jnp.concatenate(parts, axis=1)


def pack_kernel(
    members, ident_hbm, weight_hbm, rows_hbm, send_hbm, place_hbm, ident_s, weight_s, rows_s, place_s, send_s, sems
):
    count, width = rows_s.shape
    devices = send_s.shape[0]
    each = devices * CAP
    get_ident = pltpu.make_async_copy(ident_hbm, ident_s, sems.at[0])
    get_weight = pltpu.make_async_copy(weight_hbm, weight_s, sems.at[1])
    get_ident.start()
    get_weight.start()
    get_rows = []
    for index in range(PARTS):
        of = slice(index * count // PARTS, (index + 1) * count // PARTS)
        get_rows.append(pltpu.make_async_copy(rows_hbm.at[of, :], rows_s.at[of, :], sems.at[3 + index]))
        get_rows[-1].start()
    get_ident.wait()
    ident = ident_s[...]
    ident_col = column_of(ident)
    ranks = []
    for start in range(0, count, LANES):
        here = ident[:, start : start + LANES]
        same = ident_col == here
        earlier = iota((count, LANES), 0) < iota((count, LANES), 1) + start
        ranks.append(jnp.sum((same & earlier).astype(jnp.int32), axis=0, keepdims=True))
    member = ident % members
    within = ident // members * CAP + jnp.concatenate(ranks, axis=1)
    place = member * each + within
    place_s[0:1, :] = place
    place_s[1:2, :] = within
    place_s[2:3, :] = member
    put_place = pltpu.make_async_copy(place_s, place_hbm, sems.at[2])
    put_place.start()
    get_weight.wait()
    weight = weight_s[...].astype(F32).reshape(1, count)
    own_lane = iota((LANES, count), 0) == member
    weights = turned_back(jnp.where(own_lane, weight, F32(0.0))).astype(BF16)
    hot = (within == iota((each, count), 0)).astype(BF16)
    send_s[:, :, members * width :] = dot(hot, weights).astype(BF16).reshape(devices, CAP, LANES)
    for copy in get_rows:
        copy.wait()
    copies = []
    for index in range(members):
        hot = (place == index * each + iota((each, count), 0)).astype(BF16)
        packed = dot(hot, rows_s[...]).astype(BF16)
        first, last = index * width, (index + 1) * width
        send_s[:, :, first:last] = packed.reshape(devices, CAP, width)
        if index == members - 1:
            last = last + LANES
        copies.append(
            pltpu.make_async_copy(
                send_s.at[:, :, first:last], send_hbm.at[:, :, first:last], sems.at[3 + PARTS + index]
            )
        )
        copies[-1].start()
    put_place.wait()
    for copy in copies:
        copy.wait()


def turned_back(wide):
    parts = []
    for start in range(0, wide.shape[1], LANES):
        parts.append(jnp.transpose(wide[:, start : start + LANES]))
    return jnp.concatenate(parts, axis=0)


def pack(ident, weight, rows, devices, members):
    count, width = rows.shape
    wide = members * width + LANES

    def kernel(*refs):
        pack_kernel(members, *refs)

    return pl.pallas_call(
        kernel,
        out_shape=(
            pltpu.HBM((devices, CAP, wide), BF16),
            pltpu.HBM((3, count), jnp.int32),
        ),
        in_specs=[IN_HBM] * 3,
        out_specs=(IN_HBM, IN_HBM),
        scratch_shapes=[
            pltpu.VMEM((1, count), jnp.int32),
            pltpu.VMEM((count,), BF16),
            pltpu.VMEM((count, width), BF16),
            pltpu.VMEM((3, count), jnp.int32),
            pltpu.VMEM((devices, CAP, wide), BF16),
            pltpu.SemaphoreType.DMA((3 + PARTS + members,)),
        ],
        cost_estimate=pl.CostEstimate(
            flops=2 * devices * CAP * members * count * width, bytes_accessed=4 * MIB, transcendentals=0
        ),
        compiler_params=pltpu.CompilerParams(vmem_limit_bytes=63 * MIB),
        name="pack",
    )(ident, weight, rows)


def hot_kernel(place_ref, hot_ref):
    count, total = hot_ref.shape
    for row, first, last in ((0, 0, total - total // 5), (1, total - total // 5, total)):
        place = column_of(place_ref[row : row + 1, :])
        for start in range(first, last, LANES):
            hot = place == start - first + iota((count, LANES), 1)
            hot_ref[:, start : start + LANES] = hot.astype(BF16)


def hot_rows(place, devices, members):
    count = place.shape[1]
    total = devices * CAP * (members + 1)
    return pl.pallas_call(
        hot_kernel,
        out_shape=jax.ShapeDtypeStruct((count, total), BF16),
        in_specs=[IN_VMEM],
        out_specs=IN_VMEM,
        cost_estimate=pl.CostEstimate(flops=count * total, bytes_accessed=MIB, transcendentals=0),
        compiler_params=pltpu.CompilerParams(vmem_limit_bytes=8 * MIB),
        name="hot_rows",
    )(place)


def cluster_kernel(sharp_ref, got_ref, back_hbm, rows_s, prob_s, done_s, back_s, sems):
    members = sharp_ref.shape[1]
    devices, cap, wide = got_ref.shape
    width = (wide - LANES) // members
    each = devices * cap
    diagonal = iota((each, each), 0) == iota((each, each), 1)
    lane = iota((each, LANES), 1)
    weights = turned(got_ref[:, :, members * width :].reshape(each, LANES).astype(F32))
    scores = jnp.zeros((each, LANES), F32)
    copies = []
    grams, inverses = {}, {}

    def take(member):
        rows_s[member] = got_ref[:, :, member * width : (member + 1) * width].reshape(each, width)

    def products(member):
        grams[member] = dot(rows_s[member], rows_s[member], ((1,), (1,)))

    def weigh(member, scores):
        gram = grams[member]
        sharp = sharp_ref[0, member]
        rate = sharp * LOG2_E
        squares = jnp.where(diagonal, gram, F32(0.0))
        by_row = lax.rsqrt(jnp.sum(squares, axis=1, keepdims=True) + 1e-06) * rate
        by_col = lax.rsqrt(jnp.sum(squares, axis=0, keepdims=True) + 1e-06)
        scaled = jnp.where(diagonal, F32(0.0), gram * by_col * by_row)
        expo = weights[member : member + 1, :] * jnp.exp2(scaled - rate)
        total = jnp.sum(expo, axis=1, keepdims=True)
        prob_s[member] = expo.astype(BF16)
        inverses[member] = 1.0 / total
        return jnp.where(lane == member, jnp.log(total) + sharp, scores)

    def smooth(member, index):
        of = slice(index * BLOCK, (index + 1) * BLOCK)
        numer = dot(prob_s[member], rows_s[member, :, of])
        done_s[member, :, of] = (numer * inverses[member]).astype(BF16)

    def give(member, last):
        first = member * width
        back_s[:, :, first : first + width] = done_s[member].reshape(devices, cap, width)
        copies.append(
            pltpu.make_async_copy(
                back_s.at[:, :, first:last], back_hbm.at[:, :, first:last], sems.at[member]
            )
        )
        copies[-1].start()

    pairs = [tuple(range(at, min(at + 2, members))) for at in range(0, members, 2)]
    for turn in range(len(pairs) + 2):
        if turn < len(pairs):
            for member in pairs[turn]:
                take(member)
            for member in pairs[turn]:
                products(member)
        if 1 <= turn <= len(pairs):
            for index in range(width // BLOCK):
                for member in pairs[turn - 1]:
                    smooth(member, index)
        if turn < len(pairs):
            for member in pairs[turn]:
                scores = weigh(member, scores)
        if turn == len(pairs) - 1:
            back_s[:, :, members * width :] = scores.astype(BF16).reshape(devices, cap, LANES)
        if 1 <= turn <= len(pairs):
            for member in pairs[turn - 1]:
                give(member, wide if member == members - 1 else (member + 1) * width)
    for copy in copies:
        copy.wait()


def clusters(sharp, got):
    members = sharp.shape[1]
    devices, cap, wide = got.shape
    width = (wide - LANES) // members
    return pl.pallas_call(
        cluster_kernel,
        out_shape=pltpu.HBM(got.shape, BF16),
        in_specs=[IN_SMEM, IN_VMEM],
        out_specs=IN_HBM,
        scratch_shapes=[
            pltpu.VMEM((members, devices * cap, width), BF16),
            pltpu.VMEM((members, devices * cap, devices * cap), BF16),
            pltpu.VMEM((members, devices * cap, width), BF16),
            pltpu.VMEM(got.shape, BF16),
            pltpu.SemaphoreType.DMA((members,)),
        ],
        compiler_params=pltpu.CompilerParams(vmem_limit_bytes=20 * MIB),
        name="clusters",
    )(sharp, got)


def home_kernel(members, hot_ref, place_ref, home_ref, smooth_hbm, score_ref, rows_s, smooth_s, sems):
    blocks, count, block = smooth_s.shape
    devices, cap, wide = home_ref.shape
    width = blocks * block
    each = devices * cap
    copies = []
    for m in range(members):
        rows = home_ref[:, :, m * width : (m + 1) * width].reshape(each, width)
        rows_s[m * each : (m + 1) * each, :] = rows
    for index in range(blocks):
        rows = rows_s[:, index * block : (index + 1) * block]
        smooth_s[index] = dot(hot_ref[:, 0 : members * each], rows).astype(BF16)
        of = slice(index * block, (index + 1) * block)
        copies.append(pltpu.make_async_copy(smooth_s.at[index], smooth_hbm.at[:, of], sems.at[index]))
        copies[-1].start()
    scores = home_ref[:, :, members * width :].reshape(each, LANES)
    taken = turned(dot(hot_ref[:, members * each :], scores))
    own_lane = iota((LANES, count), 0) == place_ref[2:3, :]
    score = jnp.sum(jnp.where(own_lane, taken, F32(0.0)), axis=0, keepdims=True)
    score_ref[...] = score.astype(BF16).reshape(score_ref.shape)
    for copy in copies:
        copy.wait()


def bring_home(hot, place, home, members):
    count = hot.shape[0]
    width = (home.shape[2] - LANES) // members

    def kernel(*refs):
        home_kernel(members, *refs)

    return pl.pallas_call(
        kernel,
        out_shape=(jax.ShapeDtypeStruct((count, width), BF16), jax.ShapeDtypeStruct((count,), BF16)),
        in_specs=[IN_VMEM] * 3,
        out_specs=(IN_HBM, IN_VMEM),
        scratch_shapes=[
            pltpu.VMEM((home.shape[0] * home.shape[1] * members, width), BF16),
            pltpu.VMEM((width // BLOCK, count, BLOCK), BF16),
            pltpu.SemaphoreType.DMA((width // BLOCK,)),
        ],
        compiler_params=pltpu.CompilerParams(vmem_limit_bytes=16 * MIB),
        name="bring_home",
    )(hot, place, home)


def local(sentence_vectors, group_assignment, adjacent_importance, group_sharpness):
    devices = lax.axis_size("own")
    members = group_sharpness.shape[0]
    row_count = sentence_vectors.shape[0]
    send, place = pack(
        group_assignment.reshape(1, row_count), adjacent_importance, sentence_vectors, devices, members
    )
    got = lax.all_to_all(send, "own", split_axis=0, concat_axis=0, tiled=True)
    sharp = group_sharpness.astype(F32).reshape(1, members)
    back = clusters(sharp, got)
    hot = hot_rows(place, devices, members)
    home = lax.all_to_all(back, "own", split_axis=0, concat_axis=0, tiled=True)
    return bring_home(hot, place, home, members)


def solution(mesh):
    placed = (P("own", None), P("own", None), P("own"), P("own"))
    return jax.shard_map(
        local, mesh=mesh, in_specs=placed, out_specs=(P("own", None), P("own")), check_vma=False
    )
```

```python
import jax
import jax.numpy as jnp
from jax import lax
from jax.experimental import pallas as pl
from jax.experimental.pallas import tpu as pltpu
from jax.sharding import PartitionSpec as P

F32 = jnp.float32
BF16 = jnp.bfloat16
LANES = 128
CAP = 2
BLOCK = 256
HALVES = 2
PARTS = 2
CHUNK = 64
LOG2_E = 1.4426950408889634
MIB = 1 << 20
IN_VMEM = pl.BlockSpec(memory_space=pltpu.VMEM)
IN_HBM = pl.BlockSpec(memory_space=pltpu.HBM)


def iota(shape, dim):
    return lax.broadcasted_iota(jnp.int32, shape, dim)


def dot(a, b, contract=((1,), (0,))):
    return lax.dot_general(a, b, (contract, ((), ())), preferred_element_type=F32)


def column_of(row):
    parts = []
    for start in range(0, row.shape[1], LANES):
        wide = jnp.broadcast_to(row[:, start : start + LANES], (LANES, LANES))
        parts.append(jnp.transpose(wide))
    return jnp.concatenate(parts, axis=0)


def turned(tall):
    parts = []
    for start in range(0, tall.shape[0], LANES):
        parts.append(jnp.transpose(tall[start : start + LANES, :]))
    return jnp.concatenate(parts, axis=1)


def hot_of(row, each):
    spread = iota((each, row.shape[1]), 0).astype(F32).astype(BF16)
    hit = row.astype(F32).astype(BF16) == spread
    return jnp.where(hit, BF16(1.0), BF16(0.0))


def pack_kernel(
    members, ident_hbm, weight_hbm, rows_hbm, send_hbm, place_hbm, ident_s, weight_s, rows_s, place_s, send_s, sems
):
    count, width = rows_s.shape
    devices = send_s.shape[0]
    each = devices * CAP
    get_ident = pltpu.make_async_copy(ident_hbm, ident_s, sems.at[0])
    get_weight = pltpu.make_async_copy(weight_hbm, weight_s, sems.at[1])
    get_ident.start()
    get_weight.start()
    get_rows = []
    for index in range(PARTS):
        of = slice(index * count // PARTS, (index + 1) * count // PARTS)
        get_rows.append(pltpu.make_async_copy(rows_hbm.at[of, :], rows_s.at[of, :], sems.at[3 + index]))
        get_rows[-1].start()
    get_ident.wait()
    ident = ident_s[...]
    ident_col = column_of(ident)
    ranks = []
    for start in range(0, count, LANES):
        here = ident[:, start : start + LANES]
        same = ident_col[start : start + LANES, :] == here
        earlier = iota((LANES, LANES), 0) < iota((LANES, LANES), 1)
        rank = jnp.sum((same & earlier).astype(jnp.int32), axis=0, keepdims=True)
        if start > 0:
            before = ident_col[0:start, :] == here
            rank = rank + jnp.sum(before.astype(jnp.int32), axis=0, keepdims=True)
        ranks.append(rank)
    member = ident % members
    within = ident // members * CAP + jnp.concatenate(ranks, axis=1)
    place = member * each + within
    place_s[0:1, :] = place
    place_s[1:2, :] = within
    place_s[2:3, :] = member
    put_place = pltpu.make_async_copy(place_s, place_hbm, sems.at[2])
    put_place.start()
    get_weight.wait()
    for copy in get_rows:
        copy.wait()
    copies = []
    for index in range(members):
        hot = hot_of(jnp.where(member == index, within, -1), each)
        packed = dot(hot, rows_s[...]).astype(BF16)
        first, last = index * width, (index + 1) * width
        send_s[:, :, first:last] = packed.reshape(devices, CAP, width)
        if index == 0:
            weight = weight_s[...].astype(F32).reshape(1, count)
            own_lane = iota((LANES, count), 0) == member
            weights = turned_back(jnp.where(own_lane, weight, F32(0.0))).astype(BF16)
            hot = hot_of(within, each)
            weights = dot(hot, weights).astype(BF16).reshape(devices, CAP, LANES)
            send_s[:, :, members * width :] = weights
        if index == members - 1:
            last = last + LANES
        copies.append(
            pltpu.make_async_copy(
                send_s.at[:, :, first:last], send_hbm.at[:, :, first:last], sems.at[3 + PARTS + index]
            )
        )
        copies[-1].start()
    put_place.wait()
    for copy in copies:
        copy.wait()


def turned_back(wide):
    parts = []
    for start in range(0, wide.shape[1], LANES):
        parts.append(jnp.transpose(wide[:, start : start + LANES]))
    return jnp.concatenate(parts, axis=0)


def pack(ident, weight, rows, devices, members):
    count, width = rows.shape
    wide = members * width + LANES

    def kernel(*refs):
        pack_kernel(members, *refs)

    return pl.pallas_call(
        kernel,
        out_shape=(
            pltpu.HBM((devices, CAP, wide), BF16),
            pltpu.HBM((3, count), jnp.int32),
        ),
        in_specs=[IN_HBM] * 3,
        out_specs=(IN_HBM, IN_HBM),
        scratch_shapes=[
            pltpu.VMEM((1, count), jnp.int32),
            pltpu.VMEM((count,), BF16),
            pltpu.VMEM((count, width), BF16),
            pltpu.VMEM((3, count), jnp.int32),
            pltpu.VMEM((devices, CAP, wide), BF16),
            pltpu.SemaphoreType.DMA((3 + PARTS + members,)),
        ],
        cost_estimate=pl.CostEstimate(
            flops=2 * devices * CAP * members * count * width, bytes_accessed=4 * MIB, transcendentals=0
        ),
        compiler_params=pltpu.CompilerParams(vmem_limit_bytes=63 * MIB),
        name="pack",
    )(ident, weight, rows)


def hot_kernel(place_ref, hot_ref):
    count, total = hot_ref.shape
    for row, first, last in ((0, 0, total - total // 5), (1, total - total // 5, total)):
        place = column_of(place_ref[row : row + 1, :])
        for start in range(first, last, LANES):
            hot = place == start - first + iota((count, LANES), 1)
            hot_ref[:, start : start + LANES] = hot.astype(BF16)


def hot_rows(place, devices, members):
    count = place.shape[1]
    total = devices * CAP * (members + 1)
    return pl.pallas_call(
        hot_kernel,
        out_shape=jax.ShapeDtypeStruct((count, total), BF16),
        in_specs=[IN_VMEM],
        out_specs=IN_VMEM,
        cost_estimate=pl.CostEstimate(flops=count * total, bytes_accessed=MIB, transcendentals=0),
        compiler_params=pltpu.CompilerParams(vmem_limit_bytes=8 * MIB),
        name="hot_rows",
    )(place)


def cluster_kernel(sharp_ref, got_ref, back_hbm, rows_s, unit_s, prob_s, done_s, back_s, sems):
    members = sharp_ref.shape[0]
    devices, cap, wide = got_ref.shape
    width = (wide - LANES) // members
    each = devices * cap
    diagonal = iota((each, each), 0) == iota((each, each), 1)
    lane = iota((each, LANES), 1)
    weights = turned(got_ref[:, :, members * width :].reshape(each, LANES).astype(F32))
    scores = jnp.zeros((each, LANES), F32)
    copies = []
    grams, inverses = {}, {}

    def take(member):
        rows_s[member] = got_ref[:, :, member * width : (member + 1) * width].reshape(each, width)


    def norms(member):
        for start in range(0, each, CHUNK):
            wider = rows_s[member, start : start + CHUNK, :].astype(F32)
            square_sum = jnp.sum(wider * wider, axis=1, keepdims=True)
            unit = wider * lax.rsqrt(square_sum + 1e-06)
            unit_s[member, start : start + CHUNK, :] = unit.astype(BF16)

    def products(member):
        grams[member] = dot(unit_s[member], unit_s[member], ((1,), (1,)))

    def weigh(member, scores):
        gram = grams[member]
        sharp = sharp_ref[member : member + 1, :]
        rate = sharp * LOG2_E
        cosine = jnp.where(diagonal, F32(0.0), gram)
        expo = weights[member : member + 1, :] * jnp.exp2(rate * cosine - rate)
        total = jnp.sum(expo, axis=1, keepdims=True)
        prob_s[member] = expo.astype(BF16)
        inverses[member] = 1.0 / total
        return jnp.where(lane == member, jnp.log(total) + sharp[:, 0:LANES], scores)

    def smooth(member, index):
        of = slice(index * BLOCK, (index + 1) * BLOCK)
        numer = dot(prob_s[member], rows_s[member, :, of])
        done_s[member, :, of] = (numer * inverses[member]).astype(BF16)

    def give(member, last):
        first = member * width
        back_s[:, :, first : first + width] = done_s[member].reshape(devices, cap, width)
        copies.append(
            pltpu.make_async_copy(
                back_s.at[:, :, first:last], back_hbm.at[:, :, first:last], sems.at[member]
            )
        )
        copies[-1].start()

    pairs = [tuple(range(at, min(at + 2, members))) for at in range(0, members, 2)]
    for member in pairs[0]:
        take(member)
        norms(member)
    for turn in range(len(pairs) + 2):
        if turn < len(pairs):
            for member in pairs[turn]:
                products(member)
        if turn + 1 < len(pairs):
            for member in pairs[turn + 1]:
                take(member)
                norms(member)
        if turn < len(pairs):
            for member in pairs[turn]:
                scores = weigh(member, scores)
        if turn == len(pairs) - 1:
            back_s[:, :, members * width :] = scores.astype(BF16).reshape(devices, cap, LANES)
        if 1 <= turn <= len(pairs):
            for member in pairs[turn - 1]:
                for index in range(width // BLOCK):
                    smooth(member, index)
                give(member, wide if member == members - 1 else (member + 1) * width)
    for copy in copies:
        copy.wait()


def clusters(sharp, got):
    members = sharp.shape[0]
    devices, cap, wide = got.shape
    width = (wide - LANES) // members
    return pl.pallas_call(
        cluster_kernel,
        out_shape=pltpu.HBM(got.shape, BF16),
        in_specs=[IN_VMEM] * 2,
        out_specs=IN_HBM,
        scratch_shapes=[
            pltpu.VMEM((members, devices * cap, width), BF16),
            pltpu.VMEM((members, devices * cap, width), BF16),
            pltpu.VMEM((members, devices * cap, devices * cap), BF16),
            pltpu.VMEM((members, devices * cap, width), BF16),
            pltpu.VMEM(got.shape, BF16),
            pltpu.SemaphoreType.DMA((members,)),
        ],
        compiler_params=pltpu.CompilerParams(vmem_limit_bytes=20 * MIB),
        name="clusters",
    )(sharp, got)


def home_kernel(members, hot_ref, place_ref, home_ref, smooth_hbm, score_hbm, rows_s, smooth_s, score_s, sems):
    count, width = smooth_s.shape
    devices, cap, wide = home_ref.shape
    blocks = 2
    each = devices * cap
    scores = home_ref[:, :, members * width :].reshape(each, LANES)
    taken = turned(dot(hot_ref[:, members * each :], scores))
    own_lane = iota((LANES, count), 0) == place_ref[2:3, :]
    score = jnp.sum(jnp.where(own_lane, taken, F32(0.0)), axis=0, keepdims=True)
    score_s[...] = score.astype(BF16).reshape(score_s.shape)
    copies = [pltpu.make_async_copy(score_s, score_hbm, sems.at[blocks])]
    copies[0].start()
    for m in range(members):
        rows = home_ref[:, :, m * width : (m + 1) * width].reshape(each, width)
        rows_s[m * each : (m + 1) * each, :] = rows
    for index in range(blocks):
        of = slice(index * count // blocks, (index + 1) * count // blocks)
        smooth_s[of, :] = dot(hot_ref[of, 0 : members * each], rows_s[...]).astype(BF16)
        copies.append(pltpu.make_async_copy(smooth_s.at[of, :], smooth_hbm.at[of, :], sems.at[index]))
        copies[-1].start()
    for copy in copies:
        copy.wait()


def bring_home(hot, place, home, members):
    count = hot.shape[0]
    width = (home.shape[2] - LANES) // members

    def kernel(*refs):
        home_kernel(members, *refs)

    return pl.pallas_call(
        kernel,
        out_shape=(jax.ShapeDtypeStruct((count, width), BF16), jax.ShapeDtypeStruct((count,), BF16)),
        in_specs=[IN_VMEM] * 3,
        out_specs=(IN_HBM, IN_HBM),
        scratch_shapes=[
            pltpu.VMEM((home.shape[0] * home.shape[1] * members, width), BF16),
            pltpu.VMEM((count, width), BF16),
            pltpu.VMEM((count,), BF16),
            pltpu.SemaphoreType.DMA((HALVES + 1,)),
        ],
        compiler_params=pltpu.CompilerParams(vmem_limit_bytes=16 * MIB),
        name="bring_home",
    )(hot, place, home)


def local(sentence_vectors, group_assignment, adjacent_importance, group_sharpness):
    devices = lax.axis_size("own")
    members = group_sharpness.shape[0]
    row_count = sentence_vectors.shape[0]
    send, place = pack(
        group_assignment.reshape(1, row_count), adjacent_importance, sentence_vectors, devices, members
    )
    got = lax.all_to_all(send, "own", split_axis=0, concat_axis=0, tiled=True)
    sharp = jnp.broadcast_to(group_sharpness.astype(F32)[:, None], (members, devices * CAP))
    back = clusters(sharp, got)
    hot = hot_rows(place, devices, members)
    home = lax.all_to_all(back, "own", split_axis=0, concat_axis=0, tiled=True)
    return bring_home(hot, place, home, members)


def solution(mesh):
    placed = (P("own", None), P("own", None), P("own"), P("own"))
    return jax.shard_map(
        local, mesh=mesh, in_specs=placed, out_specs=(P("own", None), P("own")), check_vma=False
    )
```

```python
import jax
import jax.numpy as jnp
from jax import lax
from jax.experimental import pallas as pl
from jax.experimental.pallas import tpu as pltpu
from jax.sharding import PartitionSpec as P

F32 = jnp.float32
BF16 = jnp.bfloat16
LANES = 128
CAP = 2
BLOCK = 256
HALVES = 2
PARTS = 2
CHUNK = 64
LOG2_E = 1.4426950408889634
MIB = 1 << 20
IN_VMEM = pl.BlockSpec(memory_space=pltpu.VMEM)
IN_HBM = pl.BlockSpec(memory_space=pltpu.HBM)


def iota(shape, dim):
    return lax.broadcasted_iota(jnp.int32, shape, dim)


def dot(a, b, contract=((1,), (0,))):
    return lax.dot_general(a, b, (contract, ((), ())), preferred_element_type=F32)


def column_of(row):
    parts = []
    for start in range(0, row.shape[1], LANES):
        wide = jnp.broadcast_to(row[:, start : start + LANES], (LANES, LANES))
        parts.append(jnp.transpose(wide))
    return jnp.concatenate(parts, axis=0)


def turned(tall):
    parts = []
    for start in range(0, tall.shape[0], LANES):
        parts.append(jnp.transpose(tall[start : start + LANES, :]))
    return jnp.concatenate(parts, axis=1)


def hot_of(row, each):
    spread = iota((each, row.shape[1]), 0).astype(F32).astype(BF16)
    hit = row.astype(F32).astype(BF16) == spread
    return jnp.where(hit, BF16(1.0), BF16(0.0))


def pack_kernel(
    members, ident_hbm, weight_hbm, rows_hbm, send_hbm, place_hbm, ident_s, weight_s, rows_s, place_s, send_s, sems
):
    count, width = rows_s.shape
    devices = send_s.shape[0]
    each = devices * CAP
    get_ident = pltpu.make_async_copy(ident_hbm, ident_s, sems.at[0])
    get_weight = pltpu.make_async_copy(weight_hbm, weight_s, sems.at[1])
    get_ident.start()
    get_weight.start()
    get_rows = []
    for index in range(PARTS):
        of = slice(index * count // PARTS, (index + 1) * count // PARTS)
        get_rows.append(pltpu.make_async_copy(rows_hbm.at[of, :], rows_s.at[of, :], sems.at[3 + index]))
        get_rows[-1].start()
    get_ident.wait()
    ident = ident_s[...]
    ident_col = column_of(ident)
    ranks = []
    for start in range(0, count, LANES):
        here = ident[:, start : start + LANES]
        same = ident_col[start : start + LANES, :] == here
        earlier = iota((LANES, LANES), 0) < iota((LANES, LANES), 1)
        rank = jnp.sum((same & earlier).astype(jnp.int32), axis=0, keepdims=True)
        if start > 0:
            before = ident_col[0:start, :] == here
            rank = rank + jnp.sum(before.astype(jnp.int32), axis=0, keepdims=True)
        ranks.append(rank)
    member = ident % members
    within = ident // members * CAP + jnp.concatenate(ranks, axis=1)
    place = member * each + within
    place_s[0:1, :] = place
    place_s[1:2, :] = within
    place_s[2:3, :] = member
    put_place = pltpu.make_async_copy(place_s, place_hbm, sems.at[2])
    put_place.start()
    get_weight.wait()
    for copy in get_rows:
        copy.wait()
    copies = []
    for index in range(members):
        hot = hot_of(jnp.where(member == index, within, -1), each)
        packed = dot(hot, rows_s[...]).astype(BF16)
        first, last = index * width, (index + 1) * width
        send_s[:, :, first:last] = packed.reshape(devices, CAP, width)
        if index == 0:
            weight = weight_s[...].astype(F32).reshape(1, count)
            own_lane = iota((LANES, count), 0) == member
            ones = iota((LANES, count), 0) == members
            mixed = jnp.where(own_lane, weight, jnp.where(ones, F32(1.0), F32(0.0)))
            tile = dot(hot_of(within, each), turned_back(mixed).astype(BF16))
            lane, second = iota((each, LANES), 1), iota((each, LANES), 0) % CAP == 1
            counts = jnp.where((lane == members) & second, tile, F32(0.0))
            most = jnp.max(jnp.max(counts, axis=1, keepdims=True), axis=0, keepdims=True)
            tile = jnp.where(lane == members, most, tile)
            send_s[:, :, members * width :] = tile.astype(BF16).reshape(devices, CAP, LANES)
        if index == members - 1:
            last = last + LANES
        copies.append(
            pltpu.make_async_copy(
                send_s.at[:, :, first:last], send_hbm.at[:, :, first:last], sems.at[3 + PARTS + index]
            )
        )
        copies[-1].start()
    put_place.wait()
    for copy in copies:
        copy.wait()


def turned_back(wide):
    parts = []
    for start in range(0, wide.shape[1], LANES):
        parts.append(jnp.transpose(wide[:, start : start + LANES]))
    return jnp.concatenate(parts, axis=0)


def pack(ident, weight, rows, devices, members):
    count, width = rows.shape
    wide = members * width + LANES

    def kernel(*refs):
        pack_kernel(members, *refs)

    return pl.pallas_call(
        kernel,
        out_shape=(
            pltpu.HBM((devices, CAP, wide), BF16),
            pltpu.HBM((3, count), jnp.int32),
        ),
        in_specs=[IN_HBM] * 3,
        out_specs=(IN_HBM, IN_HBM),
        scratch_shapes=[
            pltpu.VMEM((1, count), jnp.int32),
            pltpu.VMEM((count,), BF16),
            pltpu.VMEM((count, width), BF16),
            pltpu.VMEM((3, count), jnp.int32),
            pltpu.VMEM((devices, CAP, wide), BF16),
            pltpu.SemaphoreType.DMA((3 + PARTS + members,)),
        ],
        cost_estimate=pl.CostEstimate(
            flops=2 * devices * CAP * members * count * width, bytes_accessed=4 * MIB, transcendentals=0
        ),
        compiler_params=pltpu.CompilerParams(vmem_limit_bytes=63 * MIB),
        name="pack",
    )(ident, weight, rows)


def hot_kernel(each, members, place_ref, full_ref, short_ref):
    count = full_ref.shape[0]
    place, within, member = place_ref[0:1, :], place_ref[1:2, :], place_ref[2:3, :]
    owner, rank = within // CAP, within % CAP
    key = jnp.where(rank == 1, owner * members + member, -members)
    key_col = column_of(key)
    extras = []
    for start in range(0, count, LANES):
        here = key[:, start : start + LANES]
        fewer = (key_col < here) & (key_col >= here - here % members)
        extras.append(jnp.sum(fewer.astype(jnp.int32), axis=0, keepdims=True))
    extra = jnp.concatenate(extras, axis=1)
    first = member // CAP * each + owner * CAP + member % CAP
    short = jnp.where(rank == 1, members // CAP * each + owner * CAP + extra, first)
    for ref, where in ((full_ref, place), (short_ref, short)):
        total = ref.shape[1] - each
        for low, high, row in ((0, total, where), (total, total + each, within)):
            spot = column_of(row)
            for start in range(low, high, LANES):
                hot = spot == start - low + iota((count, LANES), 1)
                ref[:, start : start + LANES] = hot.astype(BF16)


def hot_rows(place, devices, members):
    count = place.shape[1]
    each = devices * CAP
    shapes = [(count, each * (blocks + 1)) for blocks in (members, members // CAP + 1)]

    def kernel(*refs):
        hot_kernel(each, members, *refs)

    return pl.pallas_call(
        kernel,
        out_shape=[jax.ShapeDtypeStruct(shape, BF16) for shape in shapes],
        in_specs=[IN_VMEM],
        out_specs=[IN_VMEM] * 2,
        cost_estimate=pl.CostEstimate(
            flops=2 * count * each * members, bytes_accessed=2 * MIB, transcendentals=0
        ),
        compiler_params=pltpu.CompilerParams(vmem_limit_bytes=8 * MIB),
        name="hot_rows",
    )(place)


def cluster_kernel(
    sharp_ref, got_ref, short_hbm, full_hbm, most_ref, rows_s, unit_s, prob_s, left_s, done_s, sent_s, sems
):
    members = sharp_ref.shape[0]
    devices, cap, wide = got_ref.shape
    width = (wide - LANES) // members
    each = devices * cap
    halves = members // CAP
    lane = iota((each, LANES), 1)
    tile = got_ref[:, :, members * width :].reshape(each, LANES).astype(F32)
    crowd = jnp.where(lane == members, tile, F32(0.0))
    most = jnp.max(jnp.max(crowd, axis=1, keepdims=True), axis=0, keepdims=True)
    most_ref[...] = jnp.broadcast_to(most, most_ref.shape).astype(jnp.int32)
    crowded = jnp.max(most) > CAP

    def way(is_short):
        odd = iota((each, 1), 0) % CAP == 1
        diagonal = iota((each, each), 0) == iota((each, each), 1)
        weights = turned(tile)
        scores = jnp.zeros((each, LANES), F32)
        grams, inverses, chosen, copies = {}, {}, [], []

        def first_rows(value):
            return jnp.where(odd, pltpu.roll(value, 1, 0), value)

        def second_rows(value):
            return jnp.where(odd, value, pltpu.roll(value, each - 1, 0))

        if is_short:
            held = (second_rows(tile) > 0).astype(F32)
            before = jnp.zeros((each, 1), F32)
            for member in range(members):
                mine = held[:, member : member + 1]
                chosen.append((mine > 0) & (before == odd.astype(F32)))
                before = before + mine

        def take(member):
            rows_s[member * each : (member + 1) * each, :] = got_ref[
                :, :, member * width : (member + 1) * width
            ].reshape(each, width)
            for start in range(member * each, (member + 1) * each, CHUNK):
                wider = rows_s[start : start + CHUNK, :].astype(F32)
                square_sum = jnp.sum(wider * wider, axis=1, keepdims=True)
                unit = wider * lax.rsqrt(square_sum + 1e-06)
                unit_s[start : start + CHUNK, :] = unit.astype(BF16)

        def products(member):
            unit = unit_s[member * each : (member + 1) * each, :]
            grams[member] = dot(unit, unit, ((1,), (1,)))

        def weigh(member, scores):
            sharp = sharp_ref[member : member + 1, :]
            rate = sharp * LOG2_E
            cosine = jnp.where(diagonal, F32(0.0), grams[member])
            expo = weights[member : member + 1, :] * jnp.exp2(rate * cosine - rate)
            total = jnp.sum(expo, axis=1, keepdims=True)
            inverses[member] = 1.0 / total
            if is_short:
                half, at = member // CAP, member % CAP * each
                here = odd if member % CAP == 1 else ~odd
                left = jnp.where(here, first_rows(expo), F32(0.0))
                left_s[half, :, at : at + each] = left.astype(BF16)
                left = jnp.where(chosen[member], second_rows(expo), F32(0.0))
                left_s[halves + half, :, at : at + each] = left.astype(BF16)
            else:
                prob_s[member] = expo.astype(BF16)
            return jnp.where(lane == member, jnp.log(total) + sharp[:, 0:LANES], scores)

        def share(index, scores, is_last):
            if not is_short:
                left, inverse = prob_s[index], inverses[index]
                low, high = index * each, (index + 1) * each
            elif index < halves:
                own = range(index * CAP, (index + 1) * CAP)
                left = left_s[index]
                inverse = jnp.where(odd, first_rows(inverses[own[1]]), inverses[own[0]])
                low, high = own[0] * each, (own[-1] + 1) * each
            else:
                left = jnp.concatenate([left_s[halves + half] for half in range(halves)], axis=1)
                inverse = jnp.zeros((each, 1), F32)
                for member in range(members):
                    inverse = jnp.where(chosen[member], second_rows(inverses[member]), inverse)
                low, high = 0, members * each
            for start in range(0, width, BLOCK):
                of = slice(start, start + BLOCK)
                done_s[index, :, of] = (dot(left, rows_s[low:high, of]) * inverse).astype(BF16)
            first, last = index * width, (index + 1) * width
            sent_s[:, :, first:last] = done_s[index].reshape(devices, cap, width)
            if is_last:
                sent_s[:, :, last : last + LANES] = scores.astype(BF16).reshape(devices, cap, LANES)
                last = last + LANES
            to = short_hbm if is_short else full_hbm
            copies.append(
                pltpu.make_async_copy(
                    sent_s.at[:, :, first:last], to.at[:, :, first:last], sems.at[index]
                )
            )
            copies[-1].start()

        for half in range(halves):
            own = range(half * CAP, (half + 1) * CAP)
            for member in own:
                take(member)
            for member in own:
                products(member)
            for member in own:
                scores = weigh(member, scores)
            if half > 0:
                for index in range((half - 1) * CAP, half * CAP):
                    share(index // CAP if is_short else index, scores, False)
                    if is_short:
                        break
        if is_short:
            share(halves - 1, scores, False)
            share(halves, scores, True)
        else:
            for index in range((halves - 1) * CAP, members):
                share(index, scores, index == members - 1)
        for copy in copies:
            copy.wait()

    @pl.when(jnp.logical_not(crowded))
    def _():
        way(True)

    @pl.when(crowded)
    def _():
        way(False)


def clusters(sharp, got):
    members = sharp.shape[0]
    devices, cap, wide = got.shape
    width = (wide - LANES) // members
    each = devices * cap
    blocks = members // CAP + 1
    short = (devices, cap, blocks * width + LANES)
    return pl.pallas_call(
        cluster_kernel,
        out_shape=(
            pltpu.HBM(short, BF16),
            pltpu.HBM(got.shape, BF16),
            jax.ShapeDtypeStruct((1, LANES), jnp.int32),
        ),
        in_specs=[IN_VMEM] * 2,
        out_specs=(IN_HBM, IN_HBM, IN_VMEM),
        scratch_shapes=[
            pltpu.VMEM((members * each, width), BF16),
            pltpu.VMEM((members * each, width), BF16),
            pltpu.VMEM((members, each, each), BF16),
            pltpu.VMEM((2 * (members // CAP), each, CAP * each), BF16),
            pltpu.VMEM((members, each, width), BF16),
            pltpu.VMEM(got.shape, BF16),
            pltpu.SemaphoreType.DMA((members,)),
        ],
        compiler_params=pltpu.CompilerParams(vmem_limit_bytes=24 * MIB),
        name="clusters",
    )(sharp, got)


def home_kernel(hot_ref, place_ref, home_ref, smooth_hbm, score_hbm, rows_s, smooth_s, score_s, sems):
    count, width = smooth_s.shape
    devices, cap, wide = home_ref.shape
    blocks = HALVES
    members = (wide - LANES) // width
    each = devices * cap
    scores = home_ref[:, :, members * width :].reshape(each, LANES)
    taken = turned(dot(hot_ref[:, members * each :], scores))
    own_lane = iota((LANES, count), 0) == place_ref[2:3, :]
    score = jnp.sum(jnp.where(own_lane, taken, F32(0.0)), axis=0, keepdims=True)
    score_s[...] = score.astype(BF16).reshape(score_s.shape)
    copies = [pltpu.make_async_copy(score_s, score_hbm, sems.at[blocks])]
    copies[0].start()
    for m in range(members):
        rows = home_ref[:, :, m * width : (m + 1) * width].reshape(each, width)
        rows_s[m * each : (m + 1) * each, :] = rows
    for index in range(blocks):
        of = slice(index * count // blocks, (index + 1) * count // blocks)
        smooth_s[of, :] = dot(hot_ref[of, 0 : members * each], rows_s[...]).astype(BF16)
        copies.append(pltpu.make_async_copy(smooth_s.at[of, :], smooth_hbm.at[of, :], sems.at[index]))
        copies[-1].start()
    for copy in copies:
        copy.wait()


def bring_home(hot, place, home, width):
    count = hot.shape[0]
    members = (home.shape[2] - LANES) // width
    return pl.pallas_call(
        home_kernel,
        out_shape=(jax.ShapeDtypeStruct((count, width), BF16), jax.ShapeDtypeStruct((count,), BF16)),
        in_specs=[IN_VMEM] * 3,
        out_specs=(IN_HBM, IN_HBM),
        scratch_shapes=[
            pltpu.VMEM((home.shape[0] * home.shape[1] * members, width), BF16),
            pltpu.VMEM((count, width), BF16),
            pltpu.VMEM((count,), BF16),
            pltpu.SemaphoreType.DMA((HALVES + 1,)),
        ],
        compiler_params=pltpu.CompilerParams(vmem_limit_bytes=16 * MIB),
        name="bring_home",
    )(hot, place, home)


def local(sentence_vectors, group_assignment, adjacent_importance, group_sharpness):
    devices = lax.axis_size("own")
    members = group_sharpness.shape[0]
    row_count = sentence_vectors.shape[0]
    send, place = pack(
        group_assignment.reshape(1, row_count), adjacent_importance, sentence_vectors, devices, members
    )
    got = lax.all_to_all(send, "own", split_axis=0, concat_axis=0, tiled=True)
    sharp = jnp.broadcast_to(group_sharpness.astype(F32)[:, None], (members, devices * CAP))
    short, full, most = clusters(sharp, got)
    hot_full, hot_short = hot_rows(place, devices, members)

    def back(sent, hot):
        home = lax.all_to_all(sent, "own", split_axis=0, concat_axis=0, tiled=True)
        return tuple(bring_home(hot, place, home, sentence_vectors.shape[1]))

    return lax.cond(most[0, 0] > CAP, lambda: back(full, hot_full), lambda: back(short, hot_short))


def solution(mesh):
    placed = (P("own", None), P("own", None), P("own"), P("own"))
    return jax.shard_map(
        local, mesh=mesh, in_specs=placed, out_specs=(P("own", None), P("own")), check_vma=False
    )
```

```python
import jax
import jax.numpy as jnp
from jax import lax
from jax.experimental import pallas as pl
from jax.experimental.pallas import tpu as pltpu
from jax.sharding import PartitionSpec as P

F32 = jnp.float32
BF16 = jnp.bfloat16
LANES = 128
CAP = 2
BLOCK = 256
HALVES = 2
PARTS = 2
CHUNK = 64
LOG2_E = 1.4426950408889634
MIB = 1 << 20
IN_VMEM = pl.BlockSpec(memory_space=pltpu.VMEM)
IN_HBM = pl.BlockSpec(memory_space=pltpu.HBM)


def iota(shape, dim):
    return lax.broadcasted_iota(jnp.int32, shape, dim)


def dot(a, b, contract=((1,), (0,))):
    return lax.dot_general(a, b, (contract, ((), ())), preferred_element_type=F32)


def column_of(row):
    parts = []
    for start in range(0, row.shape[1], LANES):
        wide = jnp.broadcast_to(row[:, start : start + LANES], (LANES, LANES))
        parts.append(jnp.transpose(wide))
    return jnp.concatenate(parts, axis=0)


def turned(tall):
    parts = []
    for start in range(0, tall.shape[0], LANES):
        parts.append(jnp.transpose(tall[start : start + LANES, :]))
    return jnp.concatenate(parts, axis=1)


def hot_of(row, each):
    spread = iota((each, row.shape[1]), 0).astype(F32).astype(BF16)
    hit = row.astype(F32).astype(BF16) == spread
    return jnp.where(hit, BF16(1.0), BF16(0.0))


def pack_kernel(
    members, ident_hbm, weight_hbm, rows_hbm, send_hbm, place_hbm, ident_s, weight_s, rows_s, place_s, send_s, sems
):
    count, width = rows_s.shape
    devices = send_s.shape[0]
    each = devices * CAP
    get_ident = pltpu.make_async_copy(ident_hbm, ident_s, sems.at[0])
    get_weight = pltpu.make_async_copy(weight_hbm, weight_s, sems.at[1])
    get_ident.start()
    get_weight.start()
    get_rows = []
    for index in range(PARTS):
        of = slice(index * count // PARTS, (index + 1) * count // PARTS)
        get_rows.append(pltpu.make_async_copy(rows_hbm.at[of, :], rows_s.at[of, :], sems.at[3 + index]))
        get_rows[-1].start()
    get_ident.wait()
    ident = ident_s[...]
    ident_col = column_of(ident)
    ranks = []
    for start in range(0, count, LANES):
        here = ident[:, start : start + LANES]
        same = ident_col[start : start + LANES, :] == here
        earlier = iota((LANES, LANES), 0) < iota((LANES, LANES), 1)
        rank = jnp.sum((same & earlier).astype(jnp.int32), axis=0, keepdims=True)
        if start > 0:
            before = ident_col[0:start, :] == here
            rank = rank + jnp.sum(before.astype(jnp.int32), axis=0, keepdims=True)
        ranks.append(rank)
    member = ident % members
    within = ident // members * CAP + jnp.concatenate(ranks, axis=1)
    place = member * each + within
    place_s[0:1, :] = place
    place_s[1:2, :] = within
    place_s[2:3, :] = member
    put_place = pltpu.make_async_copy(place_s, place_hbm, sems.at[2])
    put_place.start()
    get_weight.wait()
    for copy in get_rows:
        copy.wait()
    copies = []
    for index in range(members):
        hot = hot_of(jnp.where(member == index, within, -1), each)
        packed = dot(hot, rows_s[...]).astype(BF16)
        first, last = index * width, (index + 1) * width
        send_s[:, :, first:last] = packed.reshape(devices, CAP, width)
        if index == 0:
            weight = weight_s[...].astype(F32).reshape(1, count)
            own_lane = iota((LANES, count), 0) == member
            ones = iota((LANES, count), 0) == members
            mixed = jnp.where(own_lane, weight, jnp.where(ones, F32(1.0), F32(0.0)))
            tile = dot(hot_of(within, each), turned_back(mixed).astype(BF16))
            lane, second = iota((each, LANES), 1), iota((each, LANES), 0) % CAP == 1
            counts = jnp.where((lane == members) & second, tile, F32(0.0))
            most = jnp.max(jnp.max(counts, axis=1, keepdims=True), axis=0, keepdims=True)
            tile = jnp.where(lane == members, most, tile)
            send_s[:, :, members * width :] = tile.astype(BF16).reshape(devices, CAP, LANES)
        if index == members - 1:
            last = last + LANES
        copies.append(
            pltpu.make_async_copy(
                send_s.at[:, :, first:last], send_hbm.at[:, :, first:last], sems.at[3 + PARTS + index]
            )
        )
        copies[-1].start()
    put_place.wait()
    for copy in copies:
        copy.wait()


def turned_back(wide):
    parts = []
    for start in range(0, wide.shape[1], LANES):
        parts.append(jnp.transpose(wide[:, start : start + LANES]))
    return jnp.concatenate(parts, axis=0)


def pack(ident, weight, rows, devices, members):
    count, width = rows.shape
    wide = members * width + LANES

    def kernel(*refs):
        pack_kernel(members, *refs)

    return pl.pallas_call(
        kernel,
        out_shape=(
            pltpu.HBM((devices, CAP, wide), BF16),
            pltpu.HBM((3, count), jnp.int32),
        ),
        in_specs=[IN_HBM] * 3,
        out_specs=(IN_HBM, IN_HBM),
        scratch_shapes=[
            pltpu.VMEM((1, count), jnp.int32),
            pltpu.VMEM((count,), BF16),
            pltpu.VMEM((count, width), BF16),
            pltpu.VMEM((3, count), jnp.int32),
            pltpu.VMEM((devices, CAP, wide), BF16),
            pltpu.SemaphoreType.DMA((3 + PARTS + members,)),
        ],
        cost_estimate=pl.CostEstimate(
            flops=2 * devices * CAP * members * count * width, bytes_accessed=4 * MIB, transcendentals=0
        ),
        compiler_params=pltpu.CompilerParams(vmem_limit_bytes=63 * MIB),
        name="pack",
    )(ident, weight, rows)


def hot_kernel(each, members, place_ref, full_ref, short_ref):
    count = full_ref.shape[0]
    place, within, member = place_ref[0:1, :], place_ref[1:2, :], place_ref[2:3, :]
    owner, rank = within // CAP, within % CAP
    key = jnp.where(rank == 1, owner * members + member, -members)
    key_col = column_of(key)
    extras = []
    for start in range(0, count, LANES):
        here = key[:, start : start + LANES]
        fewer = (key_col < here) & (key_col >= here - here % members)
        extras.append(jnp.sum(fewer.astype(jnp.int32), axis=0, keepdims=True))
    extra = jnp.concatenate(extras, axis=1)
    first = member // CAP * each + owner * CAP + member % CAP
    short = jnp.where(rank == 1, members // CAP * each + owner * CAP + extra, first)
    for ref, where in ((full_ref, place), (short_ref, short)):
        total = ref.shape[1] - each
        for low, high, row in ((0, total, where), (total, total + each, within)):
            spot = column_of(row)
            for start in range(low, high, LANES):
                hot = spot == start - low + iota((count, LANES), 1)
                ref[:, start : start + LANES] = hot.astype(BF16)


def hot_rows(place, devices, members):
    count = place.shape[1]
    each = devices * CAP
    shapes = [(count, each * (blocks + 1)) for blocks in (members, members // CAP + 1)]

    def kernel(*refs):
        hot_kernel(each, members, *refs)

    return pl.pallas_call(
        kernel,
        out_shape=[jax.ShapeDtypeStruct(shape, BF16) for shape in shapes],
        in_specs=[IN_VMEM],
        out_specs=[IN_VMEM] * 2,
        cost_estimate=pl.CostEstimate(
            flops=2 * count * each * members, bytes_accessed=2 * MIB, transcendentals=0
        ),
        compiler_params=pltpu.CompilerParams(vmem_limit_bytes=8 * MIB),
        name="hot_rows",
    )(place)


def cluster_kernel(
    sharp_ref, got_ref, short_hbm, full_hbm, most_ref, rows_s, unit_s, prob_s, left_s, done_s, sent_s, sems
):
    members = sharp_ref.shape[0]
    devices, cap, wide = got_ref.shape
    width = (wide - LANES) // members
    each = devices * cap
    halves = members // CAP
    lane = iota((each, LANES), 1)
    tile = got_ref[:, :, members * width :].reshape(each, LANES).astype(F32)
    crowd = jnp.where(lane == members, tile, F32(0.0))
    most = jnp.max(jnp.max(crowd, axis=1, keepdims=True), axis=0, keepdims=True)
    most_ref[...] = jnp.broadcast_to(most, most_ref.shape).astype(jnp.int32)
    crowded = jnp.max(most) > CAP

    def way(is_short):
        odd = iota((each, 1), 0) % CAP == 1
        diagonal = iota((each, each), 0) == iota((each, each), 1)
        weights = turned(tile)
        scores = jnp.zeros((each, LANES), F32)
        grams, inverses, chosen, copies = {}, {}, [], []

        def turn(value, shift):
            split = value.reshape(each // 8, 8, value.shape[1])
            return pltpu.roll(split, shift, 1).reshape(value.shape)

        def second_rows(value):
            return jnp.where(odd, value, turn(value, 7))

        if is_short:
            held = (second_rows(tile) > 0).astype(F32)
            before = jnp.zeros((each, 1), F32)
            for member in range(members):
                mine = held[:, member : member + 1]
                chosen.append((mine > 0) & (before == odd.astype(F32)))
                before = before + mine

        def take(member):
            rows_s[member * each : (member + 1) * each, :] = got_ref[
                :, :, member * width : (member + 1) * width
            ].reshape(each, width)
            for start in range(member * each, (member + 1) * each, CHUNK):
                wider = rows_s[start : start + CHUNK, :].astype(F32)
                square_sum = jnp.sum(wider * wider, axis=1, keepdims=True)
                unit = wider * lax.rsqrt(square_sum + 1e-06)
                unit_s[start : start + CHUNK, :] = unit.astype(BF16)

        def products(member):
            unit = unit_s[member * each : (member + 1) * each, :]
            grams[member] = dot(unit, unit, ((1,), (1,)))

        def weigh(member, scores):
            sharp = sharp_ref[member : member + 1, :]
            rate = sharp * LOG2_E
            cosine = jnp.where(diagonal, F32(0.0), grams[member])
            expo = weights[member : member + 1, :] * jnp.exp2(rate * cosine - rate)
            total = jnp.sum(expo, axis=1, keepdims=True)
            inverses[member] = 1.0 / total
            if is_short:
                half, at = member // CAP, member % CAP * each
                if member % CAP == 1:
                    left = jnp.where(odd, turn(expo, 1), F32(0.0))
                else:
                    left = jnp.where(odd, F32(0.0), expo)
                left_s[half, :, at : at + each] = left.astype(BF16)
                left = jnp.where(chosen[member], second_rows(expo), F32(0.0))
                left_s[halves + half, :, at : at + each] = left.astype(BF16)
            else:
                prob_s[member] = expo.astype(BF16)
            return jnp.where(lane == member, jnp.log(total) + sharp[:, 0:LANES], scores)

        def share(index, scores, is_last):
            if not is_short:
                left, inverse = prob_s[index], inverses[index]
                low, high = index * each, (index + 1) * each
            elif index < halves:
                own = range(index * CAP, (index + 1) * CAP)
                left = left_s[index]
                inverse = jnp.where(odd, turn(inverses[own[1]], 1), inverses[own[0]])
                low, high = own[0] * each, (own[-1] + 1) * each
            else:
                left = jnp.concatenate([left_s[halves + half] for half in range(halves)], axis=1)
                inverse = jnp.zeros((each, 1), F32)
                for member in range(members):
                    inverse = jnp.where(chosen[member], second_rows(inverses[member]), inverse)
                low, high = 0, members * each
            for start in range(0, width, BLOCK):
                of = slice(start, start + BLOCK)
                done_s[index, :, of] = (dot(left, rows_s[low:high, of]) * inverse).astype(BF16)
            first, last = index * width, (index + 1) * width
            sent_s[:, :, first:last] = done_s[index].reshape(devices, cap, width)
            if is_last:
                sent_s[:, :, last : last + LANES] = scores.astype(BF16).reshape(devices, cap, LANES)
                last = last + LANES
            to = short_hbm if is_short else full_hbm
            copies.append(
                pltpu.make_async_copy(
                    sent_s.at[:, :, first:last], to.at[:, :, first:last], sems.at[index]
                )
            )
            copies[-1].start()

        for half in range(halves):
            own = range(half * CAP, (half + 1) * CAP)
            for member in own:
                take(member)
                products(member)
            for member in own:
                scores = weigh(member, scores)
            if half > 0:
                for index in range((half - 1) * CAP, half * CAP):
                    share(index // CAP if is_short else index, scores, False)
                    if is_short:
                        break
        if is_short:
            share(halves - 1, scores, False)
            share(halves, scores, True)
        else:
            for index in range((halves - 1) * CAP, members):
                share(index, scores, index == members - 1)
        for copy in copies:
            copy.wait()

    @pl.when(jnp.logical_not(crowded))
    def _():
        way(True)

    @pl.when(crowded)
    def _():
        way(False)


def clusters(sharp, got):
    members = sharp.shape[0]
    devices, cap, wide = got.shape
    width = (wide - LANES) // members
    each = devices * cap
    blocks = members // CAP + 1
    short = (devices, cap, blocks * width + LANES)
    return pl.pallas_call(
        cluster_kernel,
        out_shape=(
            pltpu.HBM(short, BF16),
            pltpu.HBM(got.shape, BF16),
            jax.ShapeDtypeStruct((1, LANES), jnp.int32),
        ),
        in_specs=[IN_VMEM] * 2,
        out_specs=(IN_HBM, IN_HBM, IN_VMEM),
        scratch_shapes=[
            pltpu.VMEM((members * each, width), BF16),
            pltpu.VMEM((members * each, width), BF16),
            pltpu.VMEM((members, each, each), BF16),
            pltpu.VMEM((2 * (members // CAP), each, CAP * each), BF16),
            pltpu.VMEM((members, each, width), BF16),
            pltpu.VMEM(got.shape, BF16),
            pltpu.SemaphoreType.DMA((members,)),
        ],
        compiler_params=pltpu.CompilerParams(vmem_limit_bytes=24 * MIB),
        name="clusters",
    )(sharp, got)


def home_kernel(hot_ref, place_ref, home_ref, smooth_hbm, score_hbm, rows_s, smooth_s, score_s, sems):
    count, width = smooth_s.shape
    devices, cap, wide = home_ref.shape
    blocks = HALVES
    members = (wide - LANES) // width
    each = devices * cap
    scores = home_ref[:, :, members * width :].reshape(each, LANES)
    taken = turned(dot(hot_ref[:, members * each :], scores))
    own_lane = iota((LANES, count), 0) == place_ref[2:3, :]
    score = jnp.sum(jnp.where(own_lane, taken, F32(0.0)), axis=0, keepdims=True)
    score_s[...] = score.astype(BF16).reshape(score_s.shape)
    copies = [pltpu.make_async_copy(score_s, score_hbm, sems.at[blocks])]
    copies[0].start()
    for m in range(members):
        rows = home_ref[:, :, m * width : (m + 1) * width].reshape(each, width)
        rows_s[m * each : (m + 1) * each, :] = rows
    for index in range(blocks):
        of = slice(index * count // blocks, (index + 1) * count // blocks)
        smooth_s[of, :] = dot(hot_ref[of, 0 : members * each], rows_s[...]).astype(BF16)
        copies.append(pltpu.make_async_copy(smooth_s.at[of, :], smooth_hbm.at[of, :], sems.at[index]))
        copies[-1].start()
    for copy in copies:
        copy.wait()


def bring_home(hot, place, home, width):
    count = hot.shape[0]
    members = (home.shape[2] - LANES) // width
    return pl.pallas_call(
        home_kernel,
        out_shape=(jax.ShapeDtypeStruct((count, width), BF16), jax.ShapeDtypeStruct((count,), BF16)),
        in_specs=[IN_VMEM] * 3,
        out_specs=(IN_HBM, IN_HBM),
        scratch_shapes=[
            pltpu.VMEM((home.shape[0] * home.shape[1] * members, width), BF16),
            pltpu.VMEM((count, width), BF16),
            pltpu.VMEM((count,), BF16),
            pltpu.SemaphoreType.DMA((HALVES + 1,)),
        ],
        compiler_params=pltpu.CompilerParams(vmem_limit_bytes=16 * MIB),
        name="bring_home",
    )(hot, place, home)


def local(sentence_vectors, group_assignment, adjacent_importance, group_sharpness):
    devices = lax.axis_size("own")
    members = group_sharpness.shape[0]
    row_count = sentence_vectors.shape[0]
    send, place = pack(
        group_assignment.reshape(1, row_count), adjacent_importance, sentence_vectors, devices, members
    )
    got = lax.all_to_all(send, "own", split_axis=0, concat_axis=0, tiled=True)
    sharp = jnp.broadcast_to(group_sharpness.astype(F32)[:, None], (members, devices * CAP))
    short, full, most = clusters(sharp, got)
    hot_full, hot_short = hot_rows(place, devices, members)

    def back(sent, hot):
        home = lax.all_to_all(sent, "own", split_axis=0, concat_axis=0, tiled=True)
        return tuple(bring_home(hot, place, home, sentence_vectors.shape[1]))

    return lax.cond(most[0, 0] > CAP, lambda: back(full, hot_full), lambda: back(short, hot_short))


def solution(mesh):
    placed = (P("own", None), P("own", None), P("own"), P("own"))
    return jax.shard_map(
        local, mesh=mesh, in_specs=placed, out_specs=(P("own", None), P("own")), check_vma=False
    )
```

```python
import jax
import jax.numpy as jnp
from jax import lax
from jax.experimental import pallas as pl
from jax.experimental.pallas import tpu as pltpu
from jax.sharding import PartitionSpec as P

F32 = jnp.float32
BF16 = jnp.bfloat16
LANES = 128
CAP = 2
BLOCK = 256
HALVES = 2
PARTS = 2
CHUNK = 64
LOG2_E = 1.4426950408889634
MIB = 1 << 20
IN_VMEM = pl.BlockSpec(memory_space=pltpu.VMEM)
IN_HBM = pl.BlockSpec(memory_space=pltpu.HBM)


def iota(shape, dim):
    return lax.broadcasted_iota(jnp.int32, shape, dim)


def dot(a, b, contract=((1,), (0,))):
    return lax.dot_general(a, b, (contract, ((), ())), preferred_element_type=F32)


def column_of(row):
    parts = []
    for start in range(0, row.shape[1], LANES):
        wide = jnp.broadcast_to(row[:, start : start + LANES], (LANES, LANES))
        parts.append(jnp.transpose(wide))
    return jnp.concatenate(parts, axis=0)


def turned(tall):
    parts = []
    for start in range(0, tall.shape[0], LANES):
        parts.append(jnp.transpose(tall[start : start + LANES, :]))
    return jnp.concatenate(parts, axis=1)


def hot_of(row, each):
    spread = iota((each, row.shape[1]), 0).astype(F32).astype(BF16)
    hit = row.astype(F32).astype(BF16) == spread
    return jnp.where(hit, BF16(1.0), BF16(0.0))


def pack_kernel(
    members, ident_hbm, weight_hbm, rows_hbm, send_hbm, place_hbm, ident_s, weight_s, rows_s, place_s, send_s, sems
):
    count, width = rows_s.shape
    devices = send_s.shape[0]
    each = devices * CAP
    get_ident = pltpu.make_async_copy(ident_hbm, ident_s, sems.at[0])
    get_weight = pltpu.make_async_copy(weight_hbm, weight_s, sems.at[1])
    get_ident.start()
    get_weight.start()
    get_rows = []
    for index in range(PARTS):
        of = slice(index * count // PARTS, (index + 1) * count // PARTS)
        get_rows.append(pltpu.make_async_copy(rows_hbm.at[of, :], rows_s.at[of, :], sems.at[3 + index]))
        get_rows[-1].start()
    get_ident.wait()
    ident = ident_s[...]
    ident_col = column_of(ident)
    ranks = []
    for start in range(0, count, LANES):
        here = ident[:, start : start + LANES]
        same = ident_col[start : start + LANES, :] == here
        earlier = iota((LANES, LANES), 0) < iota((LANES, LANES), 1)
        rank = jnp.sum((same & earlier).astype(jnp.int32), axis=0, keepdims=True)
        if start > 0:
            before = ident_col[0:start, :] == here
            rank = rank + jnp.sum(before.astype(jnp.int32), axis=0, keepdims=True)
        ranks.append(rank)
    member = ident % members
    within = ident // members * CAP + jnp.concatenate(ranks, axis=1)
    place = member * each + within
    place_s[0:1, :] = place
    place_s[1:2, :] = within
    place_s[2:3, :] = member
    put_place = pltpu.make_async_copy(place_s, place_hbm, sems.at[2])
    put_place.start()
    get_weight.wait()
    for copy in get_rows:
        copy.wait()
    copies = []
    for index in range(members):
        hot = hot_of(jnp.where(member == index, within, -1), each)
        packed = dot(hot, rows_s[...]).astype(BF16)
        first, last = index * width, (index + 1) * width
        send_s[:, :, first:last] = packed.reshape(devices, CAP, width)
        if index == 0:
            weight = weight_s[...].astype(F32).reshape(1, count)
            own_lane = iota((LANES, count), 0) == member
            ones = iota((LANES, count), 0) == members
            mixed = jnp.where(own_lane, weight, jnp.where(ones, F32(1.0), F32(0.0)))
            tile = dot(hot_of(within, each), turned_back(mixed).astype(BF16))
            lane, second = iota((each, LANES), 1), iota((each, LANES), 0) % CAP == 1
            counts = jnp.where((lane == members) & second, tile, F32(0.0))
            most = jnp.max(jnp.max(counts, axis=1, keepdims=True), axis=0, keepdims=True)
            tile = jnp.where(lane == members, most, tile)
            send_s[:, :, members * width :] = tile.astype(BF16).reshape(devices, CAP, LANES)
        if index == members - 1:
            last = last + LANES
        copies.append(
            pltpu.make_async_copy(
                send_s.at[:, :, first:last], send_hbm.at[:, :, first:last], sems.at[3 + PARTS + index]
            )
        )
        copies[-1].start()
    put_place.wait()
    for copy in copies:
        copy.wait()


def turned_back(wide):
    parts = []
    for start in range(0, wide.shape[1], LANES):
        parts.append(jnp.transpose(wide[:, start : start + LANES]))
    return jnp.concatenate(parts, axis=0)


def pack(ident, weight, rows, devices, members):
    count, width = rows.shape
    wide = members * width + LANES

    def kernel(*refs):
        pack_kernel(members, *refs)

    return pl.pallas_call(
        kernel,
        out_shape=(
            pltpu.HBM((devices, CAP, wide), BF16),
            pltpu.HBM((3, count), jnp.int32),
        ),
        in_specs=[IN_HBM] * 3,
        out_specs=(IN_HBM, IN_HBM),
        scratch_shapes=[
            pltpu.VMEM((1, count), jnp.int32),
            pltpu.VMEM((count,), BF16),
            pltpu.VMEM((count, width), BF16),
            pltpu.VMEM((3, count), jnp.int32),
            pltpu.VMEM((devices, CAP, wide), BF16),
            pltpu.SemaphoreType.DMA((3 + PARTS + members,)),
        ],
        cost_estimate=pl.CostEstimate(
            flops=2 * devices * CAP * members * count * width, bytes_accessed=4 * MIB, transcendentals=0
        ),
        compiler_params=pltpu.CompilerParams(vmem_limit_bytes=63 * MIB),
        name="pack",
    )(ident, weight, rows)


def hot_kernel(each, members, place_ref, full_ref, short_ref):
    count = full_ref.shape[0]
    place, within, member = place_ref[0:1, :], place_ref[1:2, :], place_ref[2:3, :]
    owner, rank = within // CAP, within % CAP
    key = jnp.where(rank == 1, owner * members + member, -members)
    key_col = column_of(key)
    extras = []
    for start in range(0, count, LANES):
        here = key[:, start : start + LANES]
        fewer = (key_col < here) & (key_col >= here - here % members)
        extras.append(jnp.sum(fewer.astype(jnp.int32), axis=0, keepdims=True))
    extra = jnp.concatenate(extras, axis=1)
    first = member // CAP * each + owner * CAP + member % CAP
    short = jnp.where(rank == 1, members // CAP * each + owner * CAP + extra, first)
    for ref, where in ((full_ref, place), (short_ref, short)):
        total = ref.shape[1] - each
        for low, high, row in ((0, total, where), (total, total + each, within)):
            spot = column_of(row)
            for start in range(low, high, LANES):
                hot = spot == start - low + iota((count, LANES), 1)
                ref[:, start : start + LANES] = hot.astype(BF16)


def hot_rows(place, devices, members):
    count = place.shape[1]
    each = devices * CAP
    shapes = [(count, each * (blocks + 1)) for blocks in (members, members // CAP + 1)]

    def kernel(*refs):
        hot_kernel(each, members, *refs)

    return pl.pallas_call(
        kernel,
        out_shape=[jax.ShapeDtypeStruct(shape, BF16) for shape in shapes],
        in_specs=[IN_VMEM],
        out_specs=[IN_VMEM] * 2,
        cost_estimate=pl.CostEstimate(
            flops=2 * count * each * members, bytes_accessed=2 * MIB, transcendentals=0
        ),
        compiler_params=pltpu.CompilerParams(vmem_limit_bytes=8 * MIB),
        name="hot_rows",
    )(place)


def cluster_kernel(
    sharp_ref, got_ref, short_hbm, full_hbm, most_ref, rows_s, unit_s, prob_s, left_s, done_s, sent_s, sems
):
    members = sharp_ref.shape[0]
    devices, cap, wide = got_ref.shape
    width = (wide - LANES) // members
    each = devices * cap
    halves = members // CAP
    lane = iota((each, LANES), 1)
    tile = got_ref[:, :, members * width :].reshape(each, LANES).astype(F32)
    crowd = jnp.where(lane == members, tile, F32(0.0))
    most = jnp.max(jnp.max(crowd, axis=1, keepdims=True), axis=0, keepdims=True)
    most_ref[...] = jnp.broadcast_to(most, most_ref.shape).astype(jnp.int32)
    crowded = jnp.max(most) > CAP

    def way(is_short):
        odd = iota((each, 1), 0) % CAP == 1
        diagonal = iota((each, each), 0) == iota((each, each), 1)
        weights = turned(tile)
        scores = jnp.zeros((each, LANES), F32)
        grams, inverses, chosen, copies = {}, {}, [], []

        def turn(value, shift):
            split = value.reshape(each // 8, 8, value.shape[1])
            return pltpu.roll(split, shift, 1).reshape(value.shape)

        def second_rows(value):
            return jnp.where(odd, value, turn(value, 7))

        if is_short:
            held = (second_rows(tile) > 0).astype(F32)
            before = jnp.zeros((each, 1), F32)
            for member in range(members):
                mine = held[:, member : member + 1]
                chosen.append((mine > 0) & (before == odd.astype(F32)))
                before = before + mine

        def take(member):
            rows_s[member * each : (member + 1) * each, :] = got_ref[
                :, :, member * width : (member + 1) * width
            ].reshape(each, width)
            for start in range(member * each, (member + 1) * each, CHUNK):
                wider = rows_s[start : start + CHUNK, :].astype(F32)
                square_sum = jnp.sum(wider * wider, axis=1, keepdims=True)
                unit = wider * lax.rsqrt(square_sum + 1e-06)
                unit_s[start : start + CHUNK, :] = unit.astype(BF16)

        def products(member):
            unit = unit_s[member * each : (member + 1) * each, :]
            grams[member] = dot(unit, unit, ((1,), (1,)))

        def weigh(member, scores):
            sharp = sharp_ref[member : member + 1, :]
            rate = sharp * LOG2_E
            cosine = jnp.where(diagonal, F32(0.0), grams[member])
            expo = weights[member : member + 1, :] * jnp.exp2(rate * cosine - rate)
            total = jnp.sum(expo, axis=1, keepdims=True)
            inverses[member] = 1.0 / total
            if is_short:
                half, at = member // CAP, member % CAP * each
                if member % CAP == 1:
                    left = jnp.where(odd, turn(expo, 1), F32(0.0))
                else:
                    left = jnp.where(odd, F32(0.0), expo)
                left_s[half, :, at : at + each] = left.astype(BF16)
                left = jnp.where(chosen[member], second_rows(expo), F32(0.0))
                left_s[halves + half, :, at : at + each] = left.astype(BF16)
            else:
                prob_s[member] = expo.astype(BF16)
            return jnp.where(lane == member, jnp.log(total) + sharp[:, 0:LANES], scores)

        def share(index, scores, is_last):
            if not is_short:
                left, inverse = prob_s[index], inverses[index]
                low, high = index * each, (index + 1) * each
            elif index < halves:
                own = range(index * CAP, (index + 1) * CAP)
                left = left_s[index]
                inverse = jnp.where(odd, turn(inverses[own[1]], 1), inverses[own[0]])
                low, high = own[0] * each, (own[-1] + 1) * each
            else:
                left = jnp.concatenate([left_s[halves + half] for half in range(halves)], axis=1)
                inverse = jnp.zeros((each, 1), F32)
                for member in range(members):
                    inverse = jnp.where(chosen[member], second_rows(inverses[member]), inverse)
                low, high = 0, members * each
            for start in range(0, width, BLOCK):
                of = slice(start, start + BLOCK)
                done_s[index, :, of] = (dot(left, rows_s[low:high, of]) * inverse).astype(BF16)
            first, last = index * width, (index + 1) * width
            sent_s[:, :, first:last] = done_s[index].reshape(devices, cap, width)
            if is_last:
                sent_s[:, :, last : last + LANES] = scores.astype(BF16).reshape(devices, cap, LANES)
                last = last + LANES
            to = short_hbm if is_short else full_hbm
            copies.append(
                pltpu.make_async_copy(
                    sent_s.at[:, :, first:last], to.at[:, :, first:last], sems.at[index]
                )
            )
            copies[-1].start()

        for half in range(halves):
            own = range(half * CAP, (half + 1) * CAP)
            for member in own:
                take(member)
                products(member)
            for member in own:
                scores = weigh(member, scores)
            if half > 0:
                for index in range((half - 1) * CAP, half * CAP):
                    share(index // CAP if is_short else index, scores, False)
                    if is_short:
                        break
        if is_short:
            share(halves - 1, scores, False)
            share(halves, scores, True)
        else:
            for index in range((halves - 1) * CAP, members):
                share(index, scores, index == members - 1)
        for copy in copies:
            copy.wait()

    @pl.when(jnp.logical_not(crowded))
    def _():
        way(True)

    @pl.when(crowded)
    def _():
        way(False)


def clusters(sharp, got):
    members = sharp.shape[0]
    devices, cap, wide = got.shape
    width = (wide - LANES) // members
    each = devices * cap
    blocks = members // CAP + 1
    short = (devices, cap, blocks * width + LANES)
    return pl.pallas_call(
        cluster_kernel,
        out_shape=(
            pltpu.HBM(short, BF16),
            pltpu.HBM(got.shape, BF16),
            jax.ShapeDtypeStruct((1, LANES), jnp.int32),
        ),
        in_specs=[IN_VMEM] * 2,
        out_specs=(IN_HBM, IN_HBM, IN_VMEM),
        scratch_shapes=[
            pltpu.VMEM((members * each, width), BF16),
            pltpu.VMEM((members * each, width), BF16),
            pltpu.VMEM((members, each, each), BF16),
            pltpu.VMEM((2 * (members // CAP), each, CAP * each), BF16),
            pltpu.VMEM((members, each, width), BF16),
            pltpu.VMEM(got.shape, BF16),
            pltpu.SemaphoreType.DMA((members,)),
        ],
        compiler_params=pltpu.CompilerParams(vmem_limit_bytes=24 * MIB),
        name="clusters",
    )(sharp, got)


def home_kernel(hot_ref, place_ref, home_ref, smooth_hbm, score_hbm, rows_s, smooth_s, score_s, sems):
    count, width = smooth_s.shape
    devices, cap, wide = home_ref.shape
    blocks = HALVES
    members = (wide - LANES) // width
    each = devices * cap
    scores = home_ref[:, :, members * width :].reshape(each, LANES)
    taken = turned(dot(hot_ref[:, members * each :], scores))
    own_lane = iota((LANES, count), 0) == place_ref[2:3, :]
    score = jnp.sum(jnp.where(own_lane, taken, F32(0.0)), axis=0, keepdims=True)
    score_s[...] = score.astype(BF16).reshape(score_s.shape)
    copies = [pltpu.make_async_copy(score_s, score_hbm, sems.at[blocks])]
    copies[0].start()
    for m in range(members):
        rows = home_ref[:, :, m * width : (m + 1) * width].reshape(each, width)
        rows_s[m * each : (m + 1) * each, :] = rows
    for index in range(blocks):
        of = slice(0, count * 3 // 4) if index == 0 else slice(count * 3 // 4, count)
        smooth_s[of, :] = dot(hot_ref[of, 0 : members * each], rows_s[...]).astype(BF16)
        copies.append(pltpu.make_async_copy(smooth_s.at[of, :], smooth_hbm.at[of, :], sems.at[index]))
        copies[-1].start()
    for copy in copies:
        copy.wait()


def bring_home(hot, place, home, width):
    count = hot.shape[0]
    members = (home.shape[2] - LANES) // width
    return pl.pallas_call(
        home_kernel,
        out_shape=(jax.ShapeDtypeStruct((count, width), BF16), jax.ShapeDtypeStruct((count,), BF16)),
        in_specs=[IN_VMEM] * 3,
        out_specs=(IN_HBM, IN_HBM),
        scratch_shapes=[
            pltpu.VMEM((home.shape[0] * home.shape[1] * members, width), BF16),
            pltpu.VMEM((count, width), BF16),
            pltpu.VMEM((count,), BF16),
            pltpu.SemaphoreType.DMA((HALVES + 1,)),
        ],
        compiler_params=pltpu.CompilerParams(vmem_limit_bytes=16 * MIB),
        name="bring_home",
    )(hot, place, home)


def local(sentence_vectors, group_assignment, adjacent_importance, group_sharpness):
    devices = lax.axis_size("own")
    members = group_sharpness.shape[0]
    row_count = sentence_vectors.shape[0]
    send, place = pack(
        group_assignment.reshape(1, row_count), adjacent_importance, sentence_vectors, devices, members
    )
    got = lax.all_to_all(send, "own", split_axis=0, concat_axis=0, tiled=True)
    sharp = jnp.broadcast_to(group_sharpness.astype(F32)[:, None], (members, devices * CAP))
    short, full, most = clusters(sharp, got)
    hot_full, hot_short = hot_rows(place, devices, members)

    def back(sent, hot):
        home = lax.all_to_all(sent, "own", split_axis=0, concat_axis=0, tiled=True)
        return tuple(bring_home(hot, place, home, sentence_vectors.shape[1]))

    return lax.cond(most[0, 0] > CAP, lambda: back(full, hot_full), lambda: back(short, hot_short))


def solution(mesh):
    placed = (P("own", None), P("own", None), P("own"), P("own"))
    return jax.shard_map(
        local, mesh=mesh, in_specs=placed, out_specs=(P("own", None), P("own")), check_vma=False
    )
```
